128 devices in a mesh: dp: 4 (over x_hi, core), expert: 32 (over z, y, x_lo).
Axes of the slice: x: 4 (x_hi: 2, x_lo: 2; x = x_hi * 2 + x_lo), y: 4, z: 4, core: 2. Of those that a mesh axis runs over, the one named last changes fastest.
Arguments:
- tokens: bfloat16 [16384, 3072], P(('dp', 'expert')), may hold values from -6 to 6
- target: bfloat16 [16384, 3072], P(('dp', 'expert')), may hold values from -3 to 3
- routes: int32 [16384, 1], P(('dp', 'expert')), may hold values from 0 to 31; in each aligned block of 128 rows (0 to 127, 128 to 255, ...) at most 6 rows name the same one
- thresholds: int32 [32, 2048], P('expert', 'dp'), may hold values from 0 to 3
- enc_weight: bfloat16 [32, 3072, 2048], P('expert', None, 'dp'), may hold values from -0.109375 to 0.109375
- dec_weight: bfloat16 [32, 3072, 2048], P('expert', None, 'dp'), may hold values from -0.125 to 0.125
Outputs:
- recon: bfloat16 [16384, 3072], P(('dp', 'expert'))
- grad_enc: bfloat16 [32, 3072, 2048], P('expert', None, 'dp')
- grad_dec: bfloat16 [32, 3072, 2048], P('expert', None, 'dp')
The draws below stay inside these ranges and needn't reach their ends.
Inputs may be any that keep to these rules, and one draw needn't show every extreme that they name: `routes`: within the rows of one device no expert is named by more than 6 rows, a bound that some block reaches.
All inputs are finite; a program needn't handle non-finite values.
Results may differ from the reference program's by a relative error of at most 0.012.
Values may be sent and summed in bfloat16 or wider, within the bound.
A program may use at most 128 MiB of HBM per device.

```python
import math
import jax
import jax.numpy as jnp
import numpy as np
from jax import lax

D = 3072
F = 2048
TOK_DEV = 128
EXPERTS = 32
CAP = 6
TOKENS = 16384
N_DP = 4
N_EXPERT = 32


def place_ends(result, rng, smallest, top_value):
    longest = result.shape.index(max(result.shape))
    spots = []
    for shift in (0, 1):
        where = [jax.random.randint(jax.random.fold_in(rng, axis), (), 0, length) for axis, length in enumerate(result.shape)]
        where[longest] = (where[longest] + shift) % result.shape[longest]
        spots.append(tuple(where))
    return result.at[spots[0]].set(smallest).at[spots[1]].set(top_value)


def steps_of(own_key, shape, pieces, least, top_value):
    level = 1.0
    for position, parts in pieces:
        draws = jax.random.uniform(jax.random.fold_in(jax.random.fold_in(own_key, 6), position), (parts,), jnp.float32, least / len(pieces), top_value / len(pieces))
        level = level * jnp.repeat(jnp.exp(draws), shape[position] // parts).reshape((-1,) + (1,) * (len(shape) - 1 - position))
    return level


def shared_out(own_key, own, number, rows, number_of, top, bound, lean):
    sequence = jax.random.permutation(own_key, number_of)
    crowded, ordinary = load_shares(number_of, rows * top, bound, lean, True), load_shares(number_of, rows * top, bound, lean, False)
    places = jnp.arange(number_of)

    def named(sizes, turn):
        used = int((sizes > 0).sum())
        fixed = max(1, used // 4)
        moved = fixed + (places - fixed + turn * (used - fixed)) % max(1, number_of - fixed)
        return jnp.zeros((number_of,), jnp.int32).at[sequence[jnp.where(places < fixed, places, moved)]].set(jnp.asarray(sizes, jnp.int32))

    sizes = jnp.where(number % 4 == 0, named(crowded, number // 4), named(ordinary, number - number // 4 - 1))
    mixed = jax.random.permutation(jax.random.fold_in(own, 3), number_of)
    source_of, sink = mixed[0:number_of // 2 * 2:2], mixed[1:number_of // 2 * 2:2]
    margin = jnp.minimum(sizes[source_of] - 1, bound - sizes[sink]) // 2
    margin = jnp.where((source_of == sequence[0]) | (sink == sequence[0]) | (sizes[sink] == 0), 0, jnp.maximum(margin, 0))
    moved = jax.random.randint(jax.random.fold_in(own, 4), (number_of // 2,), 0, 1 << 20) % (margin + 1)
    sizes = sizes.at[source_of].add(-moved).at[sink].add(moved)
    items = jnp.searchsorted(jnp.cumsum(sizes), jnp.arange(rows * top), side="right").astype(jnp.int32)
    listing = items.reshape(top, rows).T
    listing = listing[jax.random.permutation(jax.random.fold_in(own, 1), rows)]
    turn = jax.random.randint(jax.random.fold_in(own, 2), (rows, 1), 0, top)
    return jnp.take_along_axis(listing, (jnp.arange(top)[None, :] + turn) % top, axis=1)


def load_shares(amount, total, most, skew, full):
    weights = [(1 << 20) // math.isqrt(grade ** skew) + 1 for grade in range(1, amount + 1)]
    largest = most if full else min(most, max(-(-total // amount), total * weights[0] // sum(weights)))
    least = 1 if total - largest >= amount - 1 else 0
    holding, spare = [largest] + [least] * (amount - 1), total - largest - least * (amount - 1)
    while spare > 0:
        movable = [i for i in range(1, amount) if holding[i] < largest] or [i for i in range(1, amount) if holding[i] < most]
        pool, budget = sum([weights[i] for i in movable]), spare
        for i in movable:
            addition = min(most - holding[i], max(1, budget * weights[i] // pool), spare)
            holding[i] = holding[i] + addition
            spare = spare - addition
    return np.array(holding)


def scatter_about(key, extent, width, most, cuts=(), held_as=jnp.bfloat16):
    drawn = width * jax.random.normal(key, extent, jnp.float32)
    if cuts:
        drawn = drawn * steps_of(key, extent, cuts, -0.22, 0.18)
    return jnp.clip(drawn, -most, most).astype(held_as)


def setup_inputs(seed: int = 0) -> dict:
    keys = jax.random.split(jax.random.key(seed), 7)
    tokens = scatter_about(keys[0], (TOKENS, D), 1.0, 6.0, ((0, 128),))
    target = scatter_about(keys[1], (TOKENS, D), 0.5, 3.0, ((0, 128),))
    routes_keys = jax.random.split(jax.random.fold_in(keys[2], 1), TOKENS // TOK_DEV)
    routes_turns = jax.random.permutation(jax.random.fold_in(keys[2], 3), TOKENS // TOK_DEV)
    routes = jax.vmap(lambda own, number: shared_out(jax.random.fold_in(keys[2], 2), own, number, TOK_DEV, EXPERTS, 1, CAP, 1))(routes_keys, routes_turns).reshape((TOKENS, 1))
    thresholds = place_ends(jax.random.randint(keys[3], (EXPERTS, F), 0, 4), jax.random.fold_in(keys[3], 1), 0, 3).astype(jnp.int32)
    enc_weight = scatter_about(keys[4], (EXPERTS, D, F), D ** -0.5, 0.109375, ((0, 32), (2, 4)))
    dec_weight = scatter_about(keys[5], (EXPERTS, D, F), F ** -0.5, 0.125, ((0, 32), (2, 4)))
    return {"tokens": tokens, "target": target, "routes": routes, "thresholds": thresholds, "enc_weight": enc_weight, "dec_weight": dec_weight}


error_scale = 0.03125


def clamp_parts(latent_pre):
    squash = jax.nn.sigmoid(4.0 * latent_pre)
    return latent_pre * squash, squash + 4.0 * latent_pre * squash * (1.0 - squash)


def reference(tokens, target, routes, thresholds, enc_weight, dec_weight):
    route_col = routes[:, 0]
    limit = N_DP * N_EXPERT * CAP

    def one_expert(expert_idx):
        row_index = jnp.nonzero(route_col == expert_idx, size=limit, fill_value=TOKENS)[0].astype(jnp.int32)
        present = (row_index < TOKENS)[:, None]
        rows_in = jnp.take(tokens, row_index, axis=0, mode="fill", fill_value=0)
        rows_target = jnp.take(target, row_index, axis=0, mode="fill", fill_value=0)
        shifts = 0.25 * thresholds[expert_idx].astype(jnp.float32)
        latent_pre = jnp.dot(rows_in, enc_weight[expert_idx], preferred_element_type=jnp.float32) - shifts
        value, derivative = clamp_parts(latent_pre)
        activity = value.astype(jnp.bfloat16)
        recon_rows = lax.dot_general(activity, dec_weight[expert_idx], (((1,), (1,)), ((), ())), preferred_element_type=jnp.float32).astype(jnp.bfloat16)
        error_rows = (recon_rows.astype(jnp.float32) - rows_target.astype(jnp.float32)) * error_scale
        error_rows = jnp.where(present, error_rows, jnp.float32(0.0)).astype(jnp.bfloat16)
        grad_act = jnp.dot(error_rows, dec_weight[expert_idx], preferred_element_type=jnp.float32)
        grad_pre = (grad_act * derivative).astype(jnp.bfloat16)
        grad_dec = lax.dot_general(error_rows, activity, (((0,), (0,)), ((), ())), preferred_element_type=jnp.float32).astype(jnp.bfloat16)
        grad_enc = lax.dot_general(rows_in, grad_pre, (((0,), (0,)), ((), ())), preferred_element_type=jnp.float32).astype(jnp.bfloat16)
        return grad_enc, grad_dec, recon_rows, row_index

    grad_enc, grad_dec, recon_rows, row_index = lax.map(one_expert, jnp.arange(EXPERTS, dtype=jnp.int32))
    recon = jnp.zeros((TOKENS, D), jnp.bfloat16).at[row_index.reshape(-1)].set(recon_rows.reshape(-1, D), mode="drop")
    return recon, grad_enc, grad_dec
```

```python
import jax
import jax.numpy as jnp
from jax import lax
from jax.sharding import PartitionSpec as P

error_scale = 0.03125
vacant_mark = 512.0


def slot_table(route_col, experts, capacity):
    choices = route_col[:, 0]
    one_hot = (choices[:, None] == jnp.arange(experts, dtype=jnp.int32)[None, :]).astype(jnp.int32)
    ranking = jnp.sum((jnp.cumsum(one_hot, axis=0) - 1) * one_hot, axis=1)
    slot_idx = choices * capacity + ranking
    positions = jnp.arange(experts * capacity, dtype=jnp.int32)
    return (positions[:, None] == slot_idx[None, :]).astype(jnp.bfloat16)


def local(tokens, target, routes, thresholds, enc_weight, dec_weight):
    experts = lax.axis_size("expert")
    per_dev = tokens.shape[0]
    features = tokens.shape[1]
    capacity = 3 * per_dev // (2 * experts)
    placing = slot_table(routes, experts, capacity)
    vacant = 1.0 - jnp.sum(placing.astype(jnp.float32), axis=1, keepdims=True)
    outbox = jnp.dot(placing, tokens, preferred_element_type=jnp.float32).astype(jnp.bfloat16)
    target_box = (
        jnp.dot(placing, target, preferred_element_type=jnp.float32) + vacant * vacant_mark
    ).astype(jnp.bfloat16)
    arrived = lax.all_to_all(
        outbox.reshape(experts, capacity, features), "expert", split_axis=0, concat_axis=0, tiled=True
    ).reshape(-1, features)
    target_rows = lax.all_to_all(
        target_box.reshape(experts, capacity, features), "expert", split_axis=0, concat_axis=0, tiled=True
    ).reshape(-1, features)
    arrived_rows = lax.all_gather(arrived, "dp", axis=0, tiled=True)
    enc_part = enc_weight[0]
    dec_part = dec_weight[0]
    shifts = 0.25 * thresholds[0].astype(jnp.float32)
    latent_pre = jnp.dot(arrived_rows, enc_part, preferred_element_type=jnp.float32) - shifts
    squash = jax.nn.sigmoid(4.0 * latent_pre)
    activity = (latent_pre * squash).astype(jnp.bfloat16)
    derivative = squash + 4.0 * latent_pre * squash * (1.0 - squash)
    partials = lax.dot_general(
        activity, dec_part, (((1,), (1,)), ((), ())), preferred_element_type=jnp.float32
    ).astype(jnp.bfloat16)
    recon_rows = lax.psum_scatter(partials, "dp", scatter_dimension=0, tiled=True)
    error_own = (recon_rows.astype(jnp.float32) - target_rows.astype(jnp.float32)) * error_scale
    error_own = jnp.where(target_rows > 0.5 * vacant_mark, 0.0, error_own).astype(jnp.bfloat16)
    error_rows = lax.all_gather(error_own, "dp", axis=0, tiled=True)
    returned = lax.all_to_all(
        recon_rows.reshape(experts, capacity, features), "expert", split_axis=0, concat_axis=0, tiled=True
    )
    recon = lax.dot_general(
        placing,
        returned.reshape(-1, features),
        (((0,), (0,)), ((), ())),
        preferred_element_type=jnp.float32,
    ).astype(jnp.bfloat16)
    grad_dec = lax.dot_general(
        error_rows, activity, (((0,), (0,)), ((), ())), preferred_element_type=jnp.float32
    ).astype(jnp.bfloat16)
    grad_act = jnp.dot(error_rows, dec_part, preferred_element_type=jnp.float32)
    grad_pre = (grad_act * derivative).astype(jnp.bfloat16)
    grad_enc = lax.dot_general(
        arrived_rows, grad_pre, (((0,), (0,)), ((), ())), preferred_element_type=jnp.float32
    ).astype(jnp.bfloat16)
    return (recon, grad_enc[None], grad_dec[None])


def solution(mesh):
    in_specs = (
        P(("dp", "expert"), None),
        P(("dp", "expert"), None),
        P(("dp", "expert"), None),
        P("expert", "dp"),
        P("expert", None, "dp"),
        P("expert", None, "dp"),
    )
    out_specs = (P(("dp", "expert"), None), P("expert", None, "dp"), P("expert", None, "dp"))
    return jax.shard_map(local, mesh=mesh, in_specs=in_specs, out_specs=out_specs, check_vma=False)
```

```python
import functools

import jax
import jax.numpy as jnp
import numpy as np
from jax import lax
from jax.experimental import pallas as pl
from jax.experimental.pallas import tpu as pltpu
from jax.sharding import PartitionSpec as P

MESH = pl.DeviceIdType.MESH
bf16 = jnp.bfloat16
f32 = jnp.float32
error_scale = 0.03125
vacant_mark = 512.0
SLOT = 8
CHUNKS = 4


def slot_table(route_col, experts):
    choices = route_col[:, 0]
    one_hot = (choices[:, None] == jnp.arange(experts, dtype=jnp.int32)[None, :]).astype(jnp.int32)
    ranking = jnp.sum((jnp.cumsum(one_hot, axis=0) - 1) * one_hot, axis=1)
    slot_idx = choices * SLOT + ranking
    positions = jnp.arange(experts * SLOT, dtype=jnp.int32)
    return (positions[:, None] == slot_idx[None, :]).astype(bf16)


def exchange_kernel(
    experts, cap,
    tok_box, tgt_box, shifts_ref, pick_ref, spread_ref, enc_hbm, dec_hbm,
    tokens_out, act_out, err_out, gpre_out, recon_in,
    tok_in, tgt_in, recon_box, tokens, errors, act, deriv, gpre, enc, dec,
    keep, sent_part, got_part, cross_out, cross_in,
    tok_s, tok_r, tgt_s, tgt_r, rec_s, rec_r,
    own_s, own_r, err_s, err_r, part_s, part_r, load_sem, out_sem,
):
    dp = lax.axis_index("dp")
    e = lax.axis_index("expert")
    core = dp % 2
    x = (dp // 2) * 2 + e % 2
    features = tokens.shape[1]
    latents = act.shape[1]
    per = experts // CHUNKS
    rows = per * cap
    span = 4 * rows

    partner = ((dp // 2) * 2 + (dp + 1) % 2, e)
    across = ((dp + 2) % 4, e)

    def odd_dp(turn):
        return ((x + turn + 2 * core) % 4 // 2) * 2 + core

    def dest(k):
        return ((dp if k % 2 == 0 else odd_dp(1)), (e + k) % experts)

    def source(k):
        return ((dp if k % 2 == 0 else odd_dp(3)), (e + experts - k) % experts)

    loads = [
        pltpu.make_async_copy(enc_hbm, enc, load_sem.at[0]),
        pltpu.make_async_copy(dec_hbm, dec, load_sem.at[1]),
    ]
    for load in loads:
        load.start()

    peers = [dest(k) for k in range(1, experts)] + [source(k) for k in range(1, experts, 2)]
    peers += [partner, across]
    barrier = pltpu.get_barrier_semaphore()
    for peer in peers:
        pl.semaphore_signal(barrier, inc=1, device_id=peer, device_id_type=MESH)
    pl.semaphore_wait(barrier, len(peers))

    def remote(src, dst, s, r, to):
        copy = pltpu.make_async_remote_copy(
            src_ref=src, dst_ref=dst, send_sem=s, recv_sem=r, device_id=to, device_id_type=MESH
        )
        copy.start()
        return copy

    tok_copies, tgt_copies = {}, {}
    for box, inbox, s, r, copies in (
        (tok_box, tok_in, tok_s, tok_r, tok_copies),
        (tgt_box, tgt_in, tgt_s, tgt_r, tgt_copies),
    ):
        local = pltpu.make_async_copy(box.at[e], inbox.at[0], r.at[0])
        local.start()
        copies[0] = local
        for k in range(1, experts):
            to = dest(k)
            copies[k] = remote(box.at[to[1]], inbox.at[k], s.at[k], r.at[k], to)

    own, err, part, rec, outs = {}, {}, {}, {}, []

    def share(buf, c, s, r, copies):
        base = c * span
        mine = buf.at[pl.ds(base, rows)]
        copies[c, "across"] = remote(mine, buf.at[pl.ds(base + 2 * rows, rows)], s.at[c, 0], r.at[c, 0], across)
        copies[c, "partner"] = remote(mine, buf.at[pl.ds(base + rows, rows)], s.at[c, 1], r.at[c, 1], partner)

    def relay(buf, c, s, r, copies):
        base = c * span
        copies[c, "across"].wait_recv()
        copies[c, "relay"] = remote(
            buf.at[pl.ds(base + 2 * rows, rows)], buf.at[pl.ds(base + 3 * rows, rows)], s.at[c, 2], r.at[c, 2], partner
        )

    def step_a(c):
        for k in range(c * per, (c + 1) * per):
            if k == 0:
                tok_copies[k].wait()
            else:
                tok_copies[k].wait_recv()
        wide = tok_in[pl.ds(c * per, per)].astype(f32).reshape(per * SLOT, features).astype(bf16)
        tokens[pl.ds(c * span, rows), :] = jnp.dot(
            pick_ref[...], wide, preferred_element_type=f32
        ).astype(bf16)
        share(tokens, c, own_s, own_r, own)

    def step_b(c):
        relay(tokens, c, own_s, own_r, own)

    def step_c(c):
        own[c, "partner"].wait_recv()
        own[c, "relay"].wait_recv()
        base = c * span
        outs.append(pltpu.make_async_copy(tokens.at[pl.ds(base, span)], tokens_out.at[pl.ds(base, span)], out_sem.at[0, c]))
        outs[-1].start()
        if c == 0:
            loads[0].wait()
        tile = 256

        def encode(j, carry):
            cols = pl.ds(pl.multiple_of(j * tile, tile), tile)
            pre = jnp.dot(tokens[pl.ds(base, span), :], enc[:, cols], preferred_element_type=f32) - shifts_ref[:, cols]
            squash = jax.nn.sigmoid(4.0 * pre)
            act[pl.ds(base, span), cols] = (pre * squash).astype(bf16)
            deriv[pl.ds(base, span), cols] = squash + 4.0 * pre * squash * (1.0 - squash)
            return carry

        lax.fori_loop(0, latents // tile, encode, 0)
        outs.append(pltpu.make_async_copy(act.at[pl.ds(base, span)], act_out.at[pl.ds(base, span)], out_sem.at[1, c]))
        outs[-1].start()
        if c == 0:
            loads[1].wait()
        wide = 512

        def decode(j, carry):
            cols = pl.ds(pl.multiple_of(j * wide, wide), wide)
            p = lax.dot_general(
                act[pl.ds(base, span), :], dec[cols, :], (((1,), (1,)), ((), ())), preferred_element_type=f32
            )
            keep[c, 0, :, cols] = p[:rows]
            keep[c, 1, :, cols] = p[2 * rows : 3 * rows]
            sent_part[c, 0, :, cols] = p[rows : 2 * rows].astype(bf16)
            sent_part[c, 1, :, cols] = p[3 * rows :].astype(bf16)
            return carry

        lax.fori_loop(0, features // wide, decode, 0)
        part[c, 1] = remote(sent_part.at[c, 1], got_part.at[c, 1], part_s.at[c, 1], part_r.at[c, 1], partner)
        part[c, 0] = remote(sent_part.at[c, 0], got_part.at[c, 0], part_s.at[c, 0], part_r.at[c, 0], partner)

    def step_d(c):
        part[c, 1].wait_recv()
        cross_out[c] = (keep[c, 1] + got_part[c, 1].astype(f32)).astype(bf16)
        part[c, 2] = remote(cross_out.at[c], cross_in.at[c], part_s.at[c, 2], part_r.at[c, 2], across)

    def step_e(c):
        part[c, 0].wait_recv()
        part[c, 2].wait_recv()
        for k in range(c * per, (c + 1) * per):
            if k == 0:
                tgt_copies[k].wait()
            else:
                tgt_copies[k].wait_recv()
        recon = (keep[c, 0] + got_part[c, 0].astype(f32) + cross_in[c].astype(f32)).astype(bf16)
        wide = tgt_in[pl.ds(c * per, per)].astype(f32).reshape(per * SLOT, features).astype(bf16)
        tgt = jnp.dot(pick_ref[...], wide, preferred_element_type=f32)
        error = (recon.astype(f32) - tgt) * error_scale
        errors[pl.ds(c * span, rows), :] = jnp.where(tgt > 0.5 * vacant_mark, 0.0, error).astype(bf16)
        share(errors, c, err_s, err_r, err)
        padded = jnp.dot(spread_ref[...], recon, preferred_element_type=f32)
        recon_box[pl.ds(c * per, per)] = padded.reshape(per, SLOT, features).astype(bf16)
        for k in range(c * per, (c + 1) * per):
            if k == 0:
                local = pltpu.make_async_copy(recon_box.at[0], recon_in.at[e], rec_r.at[0])
                local.start()
                rec[0] = local
            else:
                rec[k] = remote(recon_box.at[k], recon_in.at[e], rec_s.at[k], rec_r.at[k], source(k))

    def step_f(c):
        relay(errors, c, err_s, err_r, err)

    def step_g(c):
        err[c, "partner"].wait_recv()
        err[c, "relay"].wait_recv()
        base = c * span
        outs.append(pltpu.make_async_copy(errors.at[pl.ds(base, span)], err_out.at[pl.ds(base, span)], out_sem.at[2, c]))
        outs[-1].start()
        tile = 256

        def back(j, carry):
            cols = pl.ds(pl.multiple_of(j * tile, tile), tile)
            grad_act = jnp.dot(errors[pl.ds(base, span), :], dec[:, cols], preferred_element_type=f32)
            gpre[pl.ds(base, span), cols] = (grad_act * deriv[pl.ds(base, span), cols]).astype(bf16)
            return carry

        lax.fori_loop(0, latents // tile, back, 0)
        outs.append(pltpu.make_async_copy(gpre.at[pl.ds(base, span)], gpre_out.at[pl.ds(base, span)], out_sem.at[3, c]))
        outs[-1].start()

    steps = dict(A=step_a, B=step_b, C=step_c, D=step_d, E=step_e, F=step_f, G=step_g)
    order = (
        "A0", "A1", "B0", "A2", "C0", "B1", "A3", "D0", "C1", "B2",
        "D1", "C2", "B3", "D2", "C3", "D3", "E0", "E1", "F0", "E2",
        "F1", "G0", "E3", "F2", "G1", "F3", "G2", "G3",
    )
    for name in order:
        steps[name[0]](int(name[1]))

    for k in range(1, experts):
        tok_copies[k].wait_send()
        tgt_copies[k].wait_send()
        rec[k].wait()
    rec[0].wait()
    for copies in (own, err, part):
        for copy in copies.values():
            copy.wait_send()
    for copy in outs:
        copy.wait()


def exchange(experts, cap, tok_box, tgt_box, shifts, enc, dec):
    features, latents = enc.shape
    per = experts // CHUNKS
    rows = per * cap
    total = 4 * experts * cap
    at = np.arange(rows)
    pick = np.zeros((rows, per * SLOT), np.float32)
    pick[at, at // cap * SLOT + at % cap] = 1.0
    vmem = pl.BlockSpec(memory_space=pltpu.VMEM)
    hbm = pl.BlockSpec(memory_space=pl.ANY)
    dma = pltpu.SemaphoreType.DMA
    box = pltpu.VMEM((experts, SLOT, features), bf16)
    return pl.pallas_call(
        functools.partial(exchange_kernel, experts, cap),
        out_shape=(
            jax.ShapeDtypeStruct((total, features), bf16),
            jax.ShapeDtypeStruct((total, latents), bf16),
            jax.ShapeDtypeStruct((total, features), bf16),
            jax.ShapeDtypeStruct((total, latents), bf16),
            jax.ShapeDtypeStruct((experts, SLOT, features), bf16),
        ),
        in_specs=[vmem] * 5 + [hbm] * 2,
        out_specs=(hbm, hbm, hbm, hbm, vmem),
        scratch_shapes=[
            box, box, box,
            pltpu.VMEM((total, features), bf16),
            pltpu.VMEM((total, features), bf16),
            pltpu.VMEM((total, latents), bf16),
            pltpu.VMEM((total, latents), f32),
            pltpu.VMEM((total, latents), bf16),
            pltpu.VMEM((features, latents), bf16),
            pltpu.VMEM((features, latents), bf16),
            pltpu.VMEM((CHUNKS, 2, rows, features), f32),
            pltpu.VMEM((CHUNKS, 2, rows, features), bf16),
            pltpu.VMEM((CHUNKS, 2, rows, features), bf16),
            pltpu.VMEM((CHUNKS, rows, features), bf16),
            pltpu.VMEM((CHUNKS, rows, features), bf16),
            dma((experts,)), dma((experts,)), dma((experts,)), dma((experts,)), dma((experts,)), dma((experts,)),
            dma((CHUNKS, 3)), dma((CHUNKS, 3)), dma((CHUNKS, 3)), dma((CHUNKS, 3)), dma((CHUNKS, 3)), dma((CHUNKS, 3)),
            dma((2,)), dma((4, CHUNKS)),
        ],
        compiler_params=pltpu.CompilerParams(
            collective_id=0, has_side_effects=True, vmem_limit_bytes=60 * 1024 * 1024
        ),
        name="exchange",
    )(tok_box, tgt_box, shifts, jnp.asarray(pick, bf16), jnp.asarray(pick.T, bf16), enc, dec)


def local(tokens, target, routes, thresholds, enc_weight, dec_weight):
    experts = lax.axis_size("expert")
    per_dev = tokens.shape[0]
    features = tokens.shape[1]
    capacity = 3 * per_dev // (2 * experts)
    placing = slot_table(routes, experts)
    vacant = 1.0 - jnp.sum(placing.astype(f32), axis=1, keepdims=True)
    tok_box = jnp.dot(placing, tokens, preferred_element_type=f32).astype(bf16)
    tgt_box = (jnp.dot(placing, target, preferred_element_type=f32) + vacant * vacant_mark).astype(bf16)
    shape = (experts, SLOT, features)
    shifts = 0.25 * thresholds.astype(f32)
    token_rows, activity, error_rows, grad_pre, returned = exchange(
        experts, capacity, tok_box.reshape(shape), tgt_box.reshape(shape), shifts, enc_weight[0], dec_weight[0]
    )
    recon = lax.dot_general(
        placing, returned.reshape(-1, features), (((0,), (0,)), ((), ())), preferred_element_type=f32
    ).astype(bf16)
    grad_dec = lax.dot_general(
        error_rows, activity, (((0,), (0,)), ((), ())), preferred_element_type=f32
    ).astype(bf16)
    grad_enc = lax.dot_general(
        token_rows, grad_pre, (((0,), (0,)), ((), ())), preferred_element_type=f32
    ).astype(bf16)
    return (recon, grad_enc[None], grad_dec[None])


def solution(mesh):
    in_specs = (
        P(("dp", "expert"), None),
        P(("dp", "expert"), None),
        P(("dp", "expert"), None),
        P("expert", "dp"),
        P("expert", None, "dp"),
        P("expert", None, "dp"),
    )
    out_specs = (P(("dp", "expert"), None), P("expert", None, "dp"), P("expert", None, "dp"))
    return jax.shard_map(local, mesh=mesh, in_specs=in_specs, out_specs=out_specs, check_vma=False)
```
